256 devices in a mesh: coarse: 8 (over z), fine: 32 (over x, y, core).
Axes of the slice: x: 4, y: 4, z: 8, core: 2. Of those that a mesh axis runs over, the one named last changes fastest.
Arguments:
- volume: float32 [2048, 256, 1024], P(('coarse', 'fine')), may hold values from -6 to 6
- color_params: float32 [2, 3], replicated, may hold values from -2 to 2
- depth_order: int32 [8], replicated, may hold values from 0 to 7, each once
Outputs:
- final_image: float32 [3, 256, 1024], P(None, 'fine', 'coarse')
- opacity: float32 [256, 1024], P('fine', 'coarse')
The draws below stay inside these ranges and needn't reach their ends.
Inputs may be any that keep to these rules, and one draw needn't show every extreme that they name: `depth_order`: every place 0 to 7 is held by exactly one group.
All inputs are finite; a program needn't handle non-finite values.
Results may differ from the reference program's by a relative error of at most 0.0001.
Values sent between devices are 32-bit elements; how exact they have to be, the bound alone decides.
A program may use at most 64 MiB of HBM per device.

```python
import jax
import jax.numpy as jnp
from jax import lax

COLUMNS = 1024
ROWS = 256
GROUPS = 8
GROUP_DEPTH = 256
DEPTH = 2048


def block_scale(rng, shape, shards, low, top_value):
    factor_of, own = 1.0, jax.random.fold_in(rng, 6)
    for axis_at, shards_of in shards:
        steps = jnp.exp(jax.random.uniform(jax.random.fold_in(own, axis_at), (shards_of,), jnp.float32, low / len(shards), top_value / len(shards)))
        factor_of = factor_of * jnp.repeat(steps, shape[axis_at] // shards_of).reshape([-1 if axis == axis_at else 1 for axis in range(len(shape))])
    return factor_of


def noise(own_key, dims, scale, reach, cuts=(), held_as=jnp.bfloat16):
    result = scale * jax.random.normal(own_key, dims, jnp.float32)
    if cuts:
        result = result * block_scale(own_key, dims, cuts, -0.22, 0.18)
    return jnp.clip(result, -reach, reach).astype(held_as)


def setup_inputs(seed: int = 0) -> dict:
    arg_keys = jax.random.split(jax.random.key(seed), 4)
    volume = noise(arg_keys[0], (DEPTH, ROWS, COLUMNS), 1.0, 6.0, ((0, 256),), jnp.float32)
    color_params = jnp.clip(jax.random.uniform(arg_keys[1], (2, 3), jnp.float32, -2.0, 2.0), -2.0, 2.0)
    depth_order = jax.random.permutation(arg_keys[2], GROUPS).astype(jnp.int32)
    return {"volume": volume, "color_params": color_params, "depth_order": depth_order}


def plane_terms(previous_plane, centre_plane, next_plane, color_params, sample_step):
    grad_depth = 0.5 * (next_plane - previous_plane)
    row_padded = jnp.concatenate([centre_plane[:1], centre_plane, centre_plane[-1:]], axis=0)
    grad_row = 0.5 * (row_padded[2:] - row_padded[:-2])
    col_padded = jnp.concatenate([centre_plane[:, :1], centre_plane, centre_plane[:, -1:]], axis=1)
    grad_col = 0.5 * (col_padded[:, 2:] - col_padded[:, :-2])
    lit_term = (2.0 * grad_depth + grad_row + 2.0 * grad_col) / 3.0
    norm_term = jnp.sqrt(grad_depth * grad_depth + grad_row * grad_row + grad_col * grad_col + 1.0)
    shading = 0.35 + 0.65 * jnp.abs(lit_term) / norm_term
    slopes = color_params[0][:, None, None]
    offsets = color_params[1][:, None, None]
    emitted = 3.0 * shading[None] * jax.nn.sigmoid(slopes * centre_plane[None] + offsets)
    optical = 0.25 * centre_plane * centre_plane * sample_step
    return (emitted, optical)

def march_slab(padded, color_params, sample_step, radiance, depth_sum):
    plane_count = padded.shape[0] - 2

    def advance(plane_index, state_pair):
        radiance_now, depth_now = state_pair
        previous_plane = lax.dynamic_index_in_dim(padded, plane_index, 0, keepdims=False)
        centre_plane = lax.dynamic_index_in_dim(padded, plane_index + 1, 0, keepdims=False)
        next_plane = lax.dynamic_index_in_dim(padded, plane_index + 2, 0, keepdims=False)
        emitted, optical = plane_terms(previous_plane, centre_plane, next_plane, color_params, sample_step)
        weight = jnp.exp(-depth_now) * -jnp.expm1(-optical)
        return (radiance_now + weight[None] * emitted, depth_now + optical)
    return lax.fori_loop(0, plane_count, advance, (radiance, depth_sum))

def reference(volume, color_params, depth_order):
    groups_view = volume.reshape(GROUPS, GROUP_DEPTH, ROWS, COLUMNS)
    sample_step = 4.0 / DEPTH
    radiance = jnp.zeros((3, ROWS, COLUMNS), jnp.float32)
    depth_sum = jnp.zeros((ROWS, COLUMNS), jnp.float32)
    labels = jnp.arange(GROUPS, dtype=jnp.int32)
    for depth_place in range(GROUPS):
        chosen = jnp.sum(jnp.where(depth_order == depth_place, labels, 0)).astype(jnp.int32)
        group_slab = lax.dynamic_index_in_dim(groups_view, chosen, 0, keepdims=False)
        padded = jnp.concatenate([group_slab[:1], group_slab, group_slab[-1:]], axis=0)
        radiance, depth_sum = march_slab(padded, color_params, sample_step, radiance, depth_sum)
    return (radiance, -jnp.expm1(-depth_sum))
```

```python
import functools

import jax
import jax.numpy as jnp
from jax import lax
from jax.experimental import pallas as pl
from jax.experimental.pallas import tpu as pltpu
from jax.sharding import PartitionSpec as P

MESH = pl.DeviceIdType.MESH
NX, NY, NZ = 4, 4, 8
PLANES, ROWS, COLS = 8, 256, 1024
TILES = COLS // 128
SLOTS, UNITS = 4, 16
LAG = 2


def flip1(i):
    return i + 1 - 2 * (i % 2)


def pick(base, q):
    return jnp.where(q == 0, (base + 2) % 4, jnp.where(q == 1, flip1(base), jnp.where(q == 2, 3 - base, base)))


def kernel(step_size, par, order, vol, out, buf, part, prec, rec1, rec2, x1rec, x2rec, zrec,
           edge_sem, inner_sem, fill_sem, halo_send, hl_recv, hu_recv, c_send, c_recv,
           y1_send, y1_recv, y2_send, y2_recv, x1_send, x1_recv, x2_send, x2_recv, z_send, z_recv, gossip):
    z = lax.axis_index("coarse")
    f = lax.axis_index("fine")
    x, y, c = f // 8, (f // 2) % 4, f % 2
    ring = z // 2

    def at(xx, yy, cc):
        return (z, xx * 8 + yy * 2 + cc)

    partner = at(x, y, 1 - c)
    y_pair, y_cross = at(x, flip1(y), c), at(x, 3 - y, c)
    x_pair, x_cross = at(flip1(x), y, c), at(3 - x, y, c)
    z_near = (((z + 1) % NZ, f), ((z + NZ - 1) % NZ, f))

    def signal(sem, device):
        pl.semaphore_signal(sem, inc=1, device_id=device, device_id_type=MESH)

    barrier = pltpu.get_barrier_semaphore()

    @pl.when(f > 0)
    def _():
        signal(barrier, (z, f - 1))

    @pl.when(f < 31)
    def _():
        signal(barrier, (z, f + 1))

    for device in (y_pair, y_cross, x_pair, x_cross) + z_near:
        signal(barrier, device)

    def load(first, count, j, sem):
        return pltpu.make_async_copy(
            vol.at[pl.ds(first, count), :, pl.ds(j * 128, 128)],
            buf.at[pl.ds(first + 1, count), j + 1, pl.ds(8, ROWS), :],
            sem,
        )

    for first in (0, PLANES - 1):
        for j in range(TILES):
            load(first, 1, j, edge_sem.at[(first > 0) * TILES + j]).start()
    for j in range(TILES):
        load(1, PLANES - 2, j, inner_sem.at[j]).start()
    for first in (0, PLANES - 1):
        for j in range(TILES):
            load(first, 1, j, edge_sem.at[(first > 0) * TILES + j]).wait()

    neighbours = jnp.where(f > 0, 1, 0) + jnp.where(f < 31, 1, 0)
    pl.semaphore_wait(barrier, 6 + neighbours)

    def send(src, dst, send_sem, recv_sem, device):
        return pltpu.make_async_remote_copy(
            src_ref=src, dst_ref=dst, send_sem=send_sem, recv_sem=recv_sem, device_id=device, device_id_type=MESH
        )

    def first_tile(q):
        return 2 * ((ring + 1 + q) % 4)

    body_rows = pl.ds(8, ROWS)

    def halo(src_plane, dst_plane, recv, q, device):
        tiles = pl.ds(1 + first_tile(q), 2)
        return send(
            buf.at[src_plane, tiles, body_rows, :], buf.at[dst_plane, tiles, body_rows, :], halo_send, recv.at[q], device
        )

    def halo_down(q):
        return halo(1, PLANES + 1, hu_recv, q, (z, f - 1))

    def halo_up(q):
        return halo(PLANES, 0, hl_recv, q, (z, f + 1))

    @pl.loop(0, SLOTS)
    def _(q):
        @pl.when(f > 0)
        def _():
            halo_down(q).start()

        @pl.when(f < 31)
        def _():
            halo_up(q).start()

    for device in z_near:
        signal(gossip.at[0], device)

    def fill(src, dst):
        copy = pltpu.make_async_copy(
            buf.at[src, pl.ds(1, TILES), body_rows, :], buf.at[dst, pl.ds(1, TILES), body_rows, :], fill_sem
        )
        copy.start()
        copy.wait()

    @pl.when(f == 0)
    def _():
        fill(1, 0)

    @pl.when(f == 31)
    def _():
        fill(PLANES, PLANES + 1)

    for j in range(TILES):
        load(1, PLANES - 2, j, inner_sem.at[j]).wait()

    inner = pl.ds(1, PLANES)
    buf[inner, 1 : TILES + 1, 7:8, :] = buf[inner, 1 : TILES + 1, 8:9, :]
    buf[inner, 1 : TILES + 1, ROWS + 8 : ROWS + 9, :] = buf[inner, 1 : TILES + 1, ROWS + 7 : ROWS + 8, :]

    @pl.loop(0, ROWS // 8)
    def _(i):
        rows = pl.ds(pl.multiple_of(8 + i * 8, 8), 8)
        buf[inner, 0, rows, :] = pltpu.roll(buf[inner, 1, rows, :], 127, 2)
        buf[inner, TILES + 1, rows, :] = pltpu.roll(buf[inner, TILES, rows, :], 1, 2)

    slopes = [0.5 * par[0, i] for i in range(3)]
    offsets = [0.5 * par[1, i] for i in range(3)]
    density = 0.25 * step_size

    def march(q, g):
        j = 1 + first_tile(q)
        tiles, lefts, rights = pl.ds(j, 2), pl.ds(j - 1, 2), pl.ds(j + 1, 2)
        shape = (2, 16, 128)
        lane = lax.broadcasted_iota(jnp.int32, shape, 2)
        first, last = lane == 0, lane == 127

        @pl.loop(0, 4)
        def _(i):
            row = pl.multiple_of(8 + (pick(x, i) * 4 + pick(y, g)) * 16, 8)
            rows, above, below = pl.ds(row, 16), pl.ds(row - 1, 16), pl.ds(row + 1, 16)
            previous = buf[0, tiles, rows, :]
            s = buf[1, tiles, rows, :]
            total = jnp.zeros(shape, jnp.float32)
            colours = [total] * 3
            depth, clear = total, total + 1.0
            for p in range(1, PLANES + 1):
                following = buf[p + 1, tiles, rows, :]
                left = jnp.where(last, buf[p, lefts, rows, :], s)
                right = jnp.where(first, buf[p, rights, rows, :], s)
                dz = following - previous
                dy = buf[p, tiles, below, :] - buf[p, tiles, above, :]
                dx = pltpu.roll(right, 127, 2) - pltpu.roll(left, 1, 2)
                lit = jnp.abs((dz + dx) * 0.65 + dy * 0.325)
                shading = 0.525 + lit * lax.rsqrt(dz * dz + dy * dy + (dx * dx + 4.0))
                optical = s * s * density
                alpha = optical * (1.0 + optical * (-0.5 + optical * (1.0 / 6.0 - optical * (1.0 / 24.0))))
                weight = clear * alpha
                clear = clear - weight
                depth = depth + optical
                lead = weight * shading
                total = total + lead
                for n in range(3):
                    colours[n] = colours[n] + lead * jnp.tanh(s * slopes[n] + offsets[n])
                previous, s = s, following
            values = [total + colours[n] for n in range(3)] + [depth]
            for half in range(2):
                for n in range(4):
                    part[half, q, g, i, n] = values[n][:, half * 8 : half * 8 + 8]

    def core_copy(q, g):
        return send(part.at[1 - c, q, g], prec.at[q, g], c_send, c_recv.at[q * 4 + g], partner)

    def y1_copy(q, g, i):
        return send(part.at[c, q, g, i], rec1.at[q, g, i], y1_send, y1_recv.at[(q * 2 + g) * 4 + i], y_pair)

    def y2_copy(q, i):
        return send(part.at[c, q, 2, i], rec2.at[q, i], y2_send, y2_recv.at[q * 4 + i], y_cross)

    def x1_copy(q, i):
        return send(part.at[c, q, 3, i], x1rec.at[q, i], x1_send, x1_recv.at[q * 2 + i], x_pair)

    def x2_copy(q):
        return send(part.at[c, q, 3, 2], x2rec.at[q], x2_send, x2_recv.at[q], x_cross)

    def z_copy(q, t):
        to = first_tile(q) + t
        return send(part.at[c, q, 3, 3, :, t], zrec.at[z], z_send, z_recv.at[z], (to, f))

    def z_arrival(source):
        return send(zrec.at[source], zrec.at[source], z_send, z_recv.at[source], (z, f))

    def merge(mine, theirs, behind):
        near, far = mine[3], theirs[3]
        keep = jnp.exp(-(1.0 - behind) * far)
        take = jnp.exp(-behind * near)
        for n in range(3):
            mine[n] = keep * mine[n] + take * theirs[n]
        mine[3] = near + far

    def in_front(flag):
        return flag.astype(jnp.float32)

    c_front = in_front(1 - c)
    y1_front, y2_front = in_front(1 - y % 2), in_front(1 - y // 2)
    x1_front, x2_front = in_front(1 - x % 2), in_front(1 - x // 2)

    @pl.loop(0, UNITS + LAG)
    def _(u):
        q, g = u // 4, u % 4
        v = u - LAG
        old_q, old_g = v // 4, v % 4

        @pl.when(u < UNITS)
        def _():
            @pl.when((g == 0) & (f > 0))
            def _():
                halo_up(q).wait_recv()

            @pl.when((g == 0) & (f < 31))
            def _():
                halo_down(q).wait_recv()

            march(q, g)

        @pl.when(v >= 0)
        def _():
            core_copy(old_q, old_g).wait_recv()

            @pl.loop(0, 4)
            def _(i):
                merge(part.at[c, old_q, old_g, i], prec.at[old_q, old_g, i], c_front)

        @pl.when(u < UNITS)
        def _():
            core_copy(q, g).start()

        @pl.when((v >= 0) & (old_g < 2))
        def _():
            @pl.loop(0, 4)
            def _(i):
                y1_copy(old_q, old_g, i).start()

        for level in range(2):
            @pl.when(u == 4 + 4 * level)
            def _():
                pl.semaphore_wait(gossip.at[level], 2)
                for device in z_near:
                    signal(gossip.at[level + 1], device)

    pl.semaphore_wait(gossip.at[2], 2)

    @pl.loop(0, SLOTS)
    def _(q):
        @pl.loop(0, 4)
        def _(i):
            y1_copy(q, 0, i).wait_recv()
            merge(part.at[c, q, 2, i], rec1.at[q, 0, i], y1_front)
            y2_copy(q, i).start()

        @pl.loop(0, 4)
        def _(i):
            mine = part.at[c, q, 3, i]
            y1_copy(q, 1, i).wait_recv()
            merge(mine, rec1.at[q, 1, i], y1_front)
            y2_copy(q, i).wait_recv()
            merge(mine, rec2.at[q, i], y2_front)

            @pl.when(i < 2)
            def _():
                x1_copy(q, i).start()

            @pl.when(i >= 2)
            def _():
                x1_copy(q, i - 2).wait_recv()
                merge(mine, x1rec.at[q, i - 2], x1_front)

            @pl.when(i == 2)
            def _():
                x2_copy(q).start()

            @pl.when(i == 3)
            def _():
                x2_copy(q).wait_recv()
                merge(mine, x2rec.at[q], x2_front)

        for t in range(2):
            @pl.when((q < SLOTS - 1) | (z % 2 != t))
            def _():
                z_copy(q, t).start()

    zrec[z] = part[c, SLOTS - 1, 3, 3, :, z % 2]

    halo_rows = buf.at[0, pl.ds(1, TILES), body_rows, :]

    @pl.when(f > 0)
    def _():
        send(halo_rows, halo_rows, halo_send, hl_recv.at[0], partner).wait_send()

    @pl.when(f < 31)
    def _():
        send(halo_rows, halo_rows, halo_send, hl_recv.at[0], partner).wait_send()

    send(prec, prec, c_send, c_recv.at[0], partner).wait_send()
    send(rec1, rec1, y1_send, y1_recv.at[0], y_pair).wait_send()
    send(rec2, rec2, y2_send, y2_recv.at[0], y_cross).wait_send()
    send(x1rec, x1rec, x1_send, x1_recv.at[0], x_pair).wait_send()
    send(x2rec, x2rec, x2_send, x2_recv.at[0], x_cross).wait_send()

    for step in range(1, NZ):
        z_arrival((z + step) % NZ).wait_recv()

    depths = [zrec[g, 3] for g in range(NZ)]
    image = [jnp.zeros((8, 128), jnp.float32)] * 3
    whole = jnp.zeros((8, 128), jnp.float32)
    for g in range(NZ):
        before = jnp.zeros((8, 128), jnp.float32)
        for h in range(NZ):
            if h != g:
                before = before + depths[h] * (order[h] < order[g]).astype(jnp.float32)
        through = jnp.exp(-before)
        for n in range(3):
            image[n] = image[n] + through * zrec[g, n]
        whole = whole + depths[g]
    for n in range(3):
        out[n] = image[n]
    out[3] = whole
    seven = zrec.at[pl.ds(0, NZ - 1)]
    send(seven, seven, z_send, z_recv.at[0], z_near[0]).wait_send()


def finish(done, img, opa):
    img[...] = done[:3]
    whole = done[3]
    tail = 1.0 - whole * (1.0 / 6.0)
    for n in (5, 4, 3, 2):
        tail = 1.0 - whole * (1.0 / n) * tail
    opa[...] = jnp.where(whole < 0.25, whole * tail, 1.0 - jnp.exp(-whole))


def body(volume, color_params, depth_order):
    cell = (4, 2, 8, 128)
    dma = pltpu.SemaphoreType.DMA
    step_size = 4.0 / (PLANES * NX * NY * 2 * NZ)
    done = pl.pallas_call(
        functools.partial(kernel, step_size),
        out_shape=jax.ShapeDtypeStruct((4, 8, 128), jnp.float32),
        in_specs=[
            pl.BlockSpec(memory_space=pltpu.SMEM),
            pl.BlockSpec(memory_space=pltpu.SMEM),
            pl.BlockSpec(memory_space=pl.ANY),
        ],
        out_specs=pl.BlockSpec(memory_space=pltpu.VMEM),
        scratch_shapes=[
            pltpu.VMEM((PLANES + 2, TILES + 2, ROWS + 16, 128), jnp.float32),
            pltpu.VMEM((2, SLOTS, 4, 4) + cell, jnp.float32),
            pltpu.VMEM((SLOTS, 4, 4) + cell, jnp.float32),
            pltpu.VMEM((SLOTS, 2, 4) + cell, jnp.float32),
            pltpu.VMEM((SLOTS, 4) + cell, jnp.float32),
            pltpu.VMEM((SLOTS, 2) + cell, jnp.float32),
            pltpu.VMEM((SLOTS,) + cell, jnp.float32),
            pltpu.VMEM((NZ, 4, 8, 128), jnp.float32),
            dma((2 * TILES,)), dma((TILES,)), dma,
            dma, dma((SLOTS,)), dma((SLOTS,)),
            dma, dma((UNITS,)),
            dma, dma((2 * UNITS,)), dma, dma((UNITS,)),
            dma, dma((2 * SLOTS,)), dma, dma((SLOTS,)),
            dma, dma((NZ,)),
            pltpu.SemaphoreType.REGULAR((3,)),
        ],
        compiler_params=pltpu.CompilerParams(collective_id=0, has_side_effects=True),
    )(color_params, depth_order, volume)

    return pl.pallas_call(
        finish,
        out_shape=(jax.ShapeDtypeStruct((3, 8, 128), jnp.float32), jax.ShapeDtypeStruct((8, 128), jnp.float32)),
    )(done)


def solution(mesh):
    return jax.shard_map(
        body,
        mesh=mesh,
        in_specs=(P(("coarse", "fine"), None, None), P(), P()),
        out_specs=(P(None, "fine", "coarse"), P("fine", "coarse")),
        check_vma=False,
    )
```
